32 devices in a mesh: groups: 2 (over y), row: 4 (over z), col: 4 (over x, core).
Axes of the slice: x: 2, y: 2, z: 4, core: 2. Of those that a mesh axis runs over, the one named last changes fastest.
Arguments:
- raw_files: bfloat16 [128, 4, 8, 12000], P(('groups', 'row'), 'col'), parts along dimension 0
- file_channels: int32 [128, 4], P(('groups', 'row'), 'col'), parts along dimension 0, may hold values from 0 to 255, as said below
- reader_counts: int32 [8, 4], P(('groups', 'row'), 'col'), parts along dimension 0, may hold values from 0 to 16, as said below
- fir_taps: float32 [32], replicated, may hold values from -1 to 1
- band_bins: int32 [64], replicated, may hold values from 1 to 1499, as said below
Outputs:
- stack: bfloat16 [512, 4, 64, 128], P(('groups', 'row'), 'col'), parts along dimension 0
The draws below stay inside these ranges and needn't reach their ends.
There are 2 independent parts, one for each index of `groups`. The reference program is written for one: setup_inputs(seed, part) draws one part's arguments, and reference() takes and returns one part's arrays. A program takes and returns all parts, laid end to end along the dimension named above; an argument that names none is the same for every part. Nothing has to cross between parts.
Inputs may be any that keep to these rules, and one draw needn't show every extreme that they name: `file_channels`: channel q belongs to owner row q // 64, column (q // 16) % 4. Every channel stands in exactly one live slot (slot below its reader's count), of a reader in its owner's column. Live slots of one reader name at most 4 channels of one owner; in every column some reader holds exactly 4 channels of every owner. Slots at or above the count hold arbitrary channel numbers. `reader_counts`: in every column some reader holds 16 live slots. `band_bins`: Distinct.
All inputs are finite; a program needn't handle non-finite values.
Results may differ from the reference program's by a relative error of at most 0.017.
Values may be sent and summed in bfloat16 or wider, within the bound.
No kernel may reach another device: no remote copies, remote signals or barrier semaphores. Data moves between devices by JAX's collectives and lax.ppermute only.
A program may use at most 64 MiB of HBM per device.

```python
import math
import jax
import jax.numpy as jnp
from jax import lax

CH_DEV = 16
REC = 8
SAMP = 12000
DEC = 4
TAPS = 32
BINS = 64
M = 3000
ROWS = 4
COLS = 4
CAP = 4
SLOTS = 16
FILE_ROWS = 64
CH = 256
COLT = 64


def draw_raw_files(key, part):
    first, second, third = jax.random.split(key, 3)
    shape = (FILE_ROWS, COLS, REC, SAMP)
    scales = jnp.exp(jax.random.uniform(second, (FILE_ROWS, COLS, REC, 1), jnp.float32, 0.0, math.log(10.0)))
    envelope = jnp.exp(jax.random.uniform(third, (SAMP // 8,), jnp.float32, 0.0, math.log(10.0)))
    envelope = jnp.repeat(envelope, 8)
    noise = jax.random.truncated_normal(first, -5.0, 5.0, shape, jnp.float32)
    return (noise * scales * envelope).astype(jnp.bfloat16)


def ingest_plan(key):
    key = jax.random.fold_in(key, 11)
    heavy_key, ticket_key, junk_key, order_key = jax.random.split(key, 4)
    per_column = ROWS * CH_DEV
    heavy = jax.random.randint(heavy_key, (COLS,), 0, ROWS)
    tickets = (ROWS - 1) * CAP
    ticket_keys = jax.random.split(ticket_key, COLS * ROWS)
    picked = jax.vmap(lambda one: jax.random.permutation(one, tickets)[:CH_DEV - CAP])(ticket_keys)
    picked = picked.reshape(COLS, ROWS, CH_DEV - CAP)
    others = picked // CAP
    others = others + (others >= heavy[:, None, None]).astype(jnp.int32)
    heavy_part = jnp.broadcast_to(heavy[:, None, None], (COLS, ROWS, CAP))
    reader_of = jnp.concatenate([heavy_part, others], axis=2).reshape(COLS, per_column).astype(jnp.int32)
    order_keys = jax.random.split(order_key, COLS)
    breaker = jax.vmap(lambda one: jax.random.permutation(one, per_column))(order_keys).astype(jnp.int32)
    ranking = reader_of * per_column + breaker
    order = jnp.argsort(ranking, axis=1, stable=True).astype(jnp.int32)
    counts = jnp.sum((reader_of[:, None, :] == jnp.arange(ROWS, dtype=jnp.int32)[None, :, None]).astype(jnp.int32), axis=2)
    starts = jnp.cumsum(counts, axis=1) - counts
    sorted_reader = jnp.take_along_axis(reader_of, order, axis=1)
    position = jnp.arange(per_column, dtype=jnp.int32)[None, :] - jnp.take_along_axis(starts, sorted_reader, axis=1)
    slot_row = sorted_reader * SLOTS + position
    column_index = jnp.arange(COLS, dtype=jnp.int32)[:, None]
    channel = (order // CH_DEV * COLS + column_index) * CH_DEV + order % CH_DEV
    junk = jax.random.randint(junk_key, (COLS, FILE_ROWS), 0, CH, jnp.int32)
    column_rows = jnp.broadcast_to(column_index, (COLS, per_column))
    lists = junk.at[column_rows, slot_row].set(channel)
    return (lists.T.astype(jnp.int32), counts.T.astype(jnp.int32))


def draw_file_channels(key, part):
    return ingest_plan(key)[0]


def draw_reader_counts(key, part):
    return ingest_plan(key)[1]


def draw_band_bins(key, part):
    key = jax.random.fold_in(key, 5)
    first, second = jax.random.split(key)
    half = M // 2
    inner = (jax.random.permutation(first, half - 3) + 2)[:BINS - 2].astype(jnp.int32)
    every = jnp.concatenate([inner, jnp.array([1, half - 1], jnp.int32)])
    return every[jax.random.permutation(second, BINS)].astype(jnp.int32)


def gaussian(rng, extent, width, limit, kind=jnp.bfloat16):
    return jnp.clip(width * jax.random.normal(rng, extent, jnp.float32), -limit, limit).astype(kind)


def setup_inputs(seed: int = 0, part: int = 0) -> dict:
    streams_of = jax.random.split(jax.random.key(seed), 6)
    own_keys = jax.random.split(jax.random.fold_in(streams_of[5], part), 6)
    return {
        "raw_files": draw_raw_files(jax.random.fold_in(jax.random.fold_in(streams_of[5], part), 71), part),
        "file_channels": draw_file_channels(jax.random.fold_in(jax.random.fold_in(streams_of[5], part), 71), part),
        "reader_counts": draw_reader_counts(jax.random.fold_in(jax.random.fold_in(streams_of[5], part), 71), part),
        "fir_taps": gaussian(streams_of[3], (TAPS,), TAPS ** -0.5, 1.0, jnp.float32),
        "band_bins": draw_band_bins(jax.random.fold_in(streams_of[5], 71), part),
    }


def whiten_block(signal, fir_taps, band_bins):
    count, records, samples = signal.shape
    length = samples // DEC
    widened = jnp.pad(signal.astype(jnp.float32), ((0, 0), (0, 0), (0, TAPS)))
    decimated = jnp.zeros((count, records, length), jnp.float32)
    for offset in range(TAPS):
        decimated = decimated + fir_taps[offset] * widened[:, :, offset:offset + DEC * length:DEC]
    decimated = decimated.astype(jnp.bfloat16)
    steps = jnp.arange(length, dtype=jnp.int32)
    product = band_bins[None, :] * steps[:, None] % length
    angle = 2.0 * math.pi / length * product.astype(jnp.float32)
    table = jnp.concatenate([jnp.cos(angle), -jnp.sin(angle)], axis=1).astype(jnp.bfloat16)
    spectra = jnp.dot(decimated.reshape(count * records, length), table, preferred_element_type=jnp.float32)
    power = lax.optimization_barrier(jnp.mean(spectra * spectra, axis=1, keepdims=True))
    white = spectra / jnp.sqrt(power + 1e-06)
    return white.reshape(count, records, 2 * BINS).astype(jnp.bfloat16)

def reference(raw_files, file_channels, reader_counts, fir_taps, band_bins):
    slot_index = jnp.arange(FILE_ROWS, dtype=jnp.int32)
    within = slot_index % SLOTS
    reader = slot_index // SLOTS
    live = within[:, None] < reader_counts[reader, :]
    target = jnp.where(live, file_channels, CH).astype(jnp.int32)
    signal = jnp.zeros((CH, REC, SAMP), jnp.bfloat16)
    signal = signal.at[target.reshape(-1)].set(raw_files.reshape(FILE_ROWS * COLS, REC, SAMP), mode='drop')
    blocks = signal.reshape(CH // CH_DEV, CH_DEV, REC, SAMP)
    white = lax.map(lambda block: whiten_block(block, fir_taps, band_bins), blocks)
    white = white.reshape(CH, REC, 2 * BINS)
    ordered = white.reshape(ROWS, COLS, CH_DEV, REC, 2 * BINS).transpose(1, 0, 2, 3, 4).reshape(CH, REC, 2 * BINS)
    right = ordered.astype(jnp.float32)
    right_re = right[:, :, :BINS]
    right_im = right[:, :, BINS:]

    def grid_row(block):
        left = block.astype(jnp.float32)
        left_re = left[:, :, :BINS]
        left_im = left[:, :, BINS:]
        real = jnp.einsum('ieb,jeb->ijb', left_re, right_re) + jnp.einsum('ieb,jeb->ijb', left_im, right_im)
        imag = jnp.einsum('ieb,jeb->ijb', left_im, right_re) - jnp.einsum('ieb,jeb->ijb', left_re, right_im)
        joined = jnp.concatenate([real, imag], axis=2) / REC
        return joined.astype(jnp.bfloat16)
    rows_of_grid = white.reshape(ROWS, COLS * CH_DEV, REC, 2 * BINS)
    result = lax.map(grid_row, rows_of_grid)
    return result.reshape(CH, COLS, COLT, 2 * BINS)
```

```python
import functools
import math

import jax
import jax.numpy as jnp
from jax import lax
from jax.experimental import pallas as pl
from jax.experimental.pallas import tpu as pltpu
from jax.sharding import PartitionSpec as P

CH_DEV = 16
DEC = 4
SPAN = 512
LANES = 128
TILE = 16
SIN = (6.283185307, -41.341702147, 81.60523051, -76.704495669, 42.014104466, -14.423992009)


def split(x):
    high = x.astype(jnp.bfloat16)
    return high, (x - high.astype(jnp.float32)).astype(jnp.bfloat16)


def turn_cos(steps, length):
    steps = steps - jnp.round(steps * (1.0 / length)) * length
    gap = 0.25 - jnp.abs(steps * (1.0 / length))
    square = gap * gap
    value = jnp.full_like(gap, SIN[-1])
    for term in SIN[-2::-1]:
        value = value * square + term
    return value * gap


def dot(a, b):
    return jnp.dot(a, b, preferred_element_type=jnp.float32)


def dot_t(a, b):
    return lax.dot_general(a, b, (((1,), (1,)), ((), ())), preferred_element_type=jnp.float32)


def iota(shape, axis):
    return lax.broadcasted_iota(jnp.int32, shape, axis)


def whiten_kernel(ncols, records, taps_count, counts, raw, taps, bins, channels, out, held, sems):
    rows, samples = raw.shape
    length = samples // DEC
    chunk = rows // sems.shape[0]
    copies = []
    for index in range(sems.shape[0]):
        part = pl.ds(index * chunk, chunk)
        copies.append(pltpu.make_async_copy(raw.at[part, :], held.at[part, :], sems.at[index]))
        copies[-1].start()
    width = out.shape[1]
    half = width // 2
    before = taps_count // DEC - 1
    depth = SPAN // DEC + before
    depth = (depth + TILE - 1) // TILE * TILE
    base = bins[...].astype(jnp.float32)
    band = jnp.concatenate([base, base], axis=1)
    quarter = jnp.where(iota((1, width), 1) < half, 0.0, 0.25 * length)
    eye = iota((width, width), 0) == iota((width, width), 1)
    band_col = jnp.sum(jnp.where(eye, band, 0.0), axis=1, keepdims=True)
    quarter_col = jnp.where(iota((width, 1), 0) < half, 0.0, 0.25 * length)
    place = iota((width, depth), 1)
    wave = turn_cos(band_col * (place - before).astype(jnp.float32) - quarter_col, length)
    wave_high, wave_low = split(wave)
    gap = iota((depth, SPAN), 1) - DEC * (iota((depth, SPAN), 0) - before)
    lane_taps = jnp.concatenate([taps[...], jnp.zeros((1, LANES - taps_count), jnp.float32)], axis=1)
    lane_taps = jnp.broadcast_to(lane_taps, (depth, LANES))
    pieces = []
    for start in range(0, SPAN, LANES):
        where = gap[:, start : start + LANES]
        found = jnp.take_along_axis(lane_taps, jnp.clip(where, 0, taps_count - 1), axis=1)
        pieces.append(jnp.where((where >= 0) & (where < taps_count), found, 0.0))
    banded = jnp.concatenate(pieces, axis=1)
    band_high, band_low = split(banded)
    table = dot(wave_high, band_high) + dot(wave_high, band_low) + dot(wave_low, band_high)
    table = jnp.concatenate(split(table), axis=0)
    early = place < before
    early_high = jnp.where(early, wave_high.astype(jnp.float32), 0.0).astype(jnp.bfloat16)
    early_low = jnp.where(early, wave_low.astype(jnp.float32), 0.0).astype(jnp.bfloat16)
    first_high, first_low = band_high[:, :LANES], band_low[:, :LANES]
    edge = dot(early_high, first_high) + dot(early_high, first_low) + dot(early_low, first_high)
    edge = jnp.concatenate(split(edge), axis=0)
    blocks = (samples + SPAN - 1) // SPAN
    turns = (iota((blocks, width), 0) * (SPAN // DEC)).astype(jnp.float32) * band
    cosine = turn_cos(turns, length)
    sine = turn_cos(turns - 0.25 * length, length)
    sign = jnp.where(iota((1, width), 1) < half, 1.0, -1.0)
    slots = rows // records
    for index in range(sems.shape[0]):
        copies[index].wait()
        part = pl.ds(index * chunk, chunk)
        along = jnp.zeros((chunk, width), jnp.float32)
        across = jnp.zeros((chunk, width), jnp.float32)
        for block in range(blocks):
            size = min(SPAN, samples - block * SPAN)
            piece = held[part, block * SPAN : block * SPAN + size]
            both = dot_t(piece, table[:, :size])
            term = both[:, :width] + both[:, width:]
            if block == 0:
                fix = dot_t(piece[:, :LANES], edge)
                along = term - fix[:, :width] - fix[:, width:]
            else:
                along = along + term * cosine[block : block + 1]
                across = across + term * sine[block : block + 1]
        spectra = along * sign - pltpu.roll(across, half, 1)
        power = jnp.mean(spectra * spectra, axis=1, keepdims=True)
        white = spectra / jnp.sqrt(power + 1e-06)
        slot = (iota((chunk, 1), 0) + index * chunk) // records
        out[part, :] = jnp.where(slot < counts[0, 0], white, 0.0).astype(out.dtype)
    owner = channels[...] // (CH_DEV * ncols)
    local = owner * CH_DEV + channels[...] % CH_DEV
    local = jnp.where(iota((1, slots), 1) < counts[0, 0], local, -1).astype(jnp.float32)
    local = jnp.broadcast_to(
        jnp.concatenate([local, jnp.zeros((1, LANES - slots), jnp.float32)], axis=1), (TILE, LANES)
    )
    source = iota((TILE, LANES), 0) * (LANES // records) + iota((TILE, LANES), 1) // records
    labels = jnp.take_along_axis(local, jnp.minimum(source, slots - 1), axis=1)
    out[rows:, :] = labels.astype(out.dtype)


def whiten(raw_files, file_channels, reader_counts, fir_taps, band_bins, ncols):
    slots, _, records, samples = raw_files.shape
    rows = slots * records
    width = 2 * band_bins.shape[0]
    chunks = 2
    vmem = pl.BlockSpec(memory_space=pltpu.VMEM)
    return pl.pallas_call(
        functools.partial(whiten_kernel, ncols, records, fir_taps.shape[0]),
        out_shape=jax.ShapeDtypeStruct((rows + TILE, width), jnp.bfloat16),
        in_specs=[
            pl.BlockSpec(memory_space=pltpu.SMEM),
            pl.BlockSpec(memory_space=pl.ANY),
            vmem,
            vmem,
            vmem,
        ],
        out_specs=vmem,
        scratch_shapes=[pltpu.VMEM((rows, samples), jnp.bfloat16), pltpu.SemaphoreType.DMA((chunks,))],
        name="whiten",
    )(
        reader_counts,
        raw_files.reshape(rows, samples),
        fir_taps.reshape(1, -1),
        band_bins.reshape(1, -1),
        file_channels.reshape(1, -1),
    )


def placing(packet, targets, records):
    rows = packet.shape[0] - TILE
    picks = []
    for group in range(rows // LANES):
        labels = packet[rows : rows + TILE, :].astype(jnp.float32)[group : group + 1]
        keys = labels * records + (iota((1, LANES), 1) % records).astype(jnp.float32)
        picks.append((targets == keys).astype(jnp.float32).astype(jnp.bfloat16))
    return jnp.concatenate(picks, axis=1)


def gather_rows(packets, targets, records):
    picks = jnp.concatenate([placing(p, targets, records) for p in packets], axis=1)
    data = jnp.concatenate([p[: p.shape[0] - TILE, :] for p in packets], axis=0)
    return dot(picks, data)


def own_kernel(records, *refs):
    packets, out = refs[:-1], refs[-1]
    count = out.shape[0]
    first = lax.axis_index("row") * count
    targets = (iota((count, 1), 0) + first).astype(jnp.float32)
    out[...] = gather_rows(packets, targets, records).astype(out.dtype)


def own_block(packets, records):
    vmem = pl.BlockSpec(memory_space=pltpu.VMEM)
    return pl.pallas_call(
        functools.partial(own_kernel, records),
        out_shape=jax.ShapeDtypeStruct((CH_DEV * records, packets[0].shape[1]), packets[0].dtype),
        in_specs=[vmem] * len(packets),
        out_specs=vmem,
        name="own",
    )(*packets)


def stack_kernel(records, nrows, ncols, *refs):
    packets = refs[:nrows]
    lefts = refs[nrows : nrows + ncols]
    out, right_re, right_im, left, left_turned, tiles, sems = refs[nrows + ncols :]
    width = out.shape[2]
    half = width // 2
    count = nrows * CH_DEV
    low = iota((1, width), 1) < half
    for start in range(0, count, 64):
        block = min(64, count - start)
        for record in range(records):
            targets = ((iota((block, 1), 0) + start) * records + record).astype(jnp.float32)
            placed = gather_rows(packets, targets, records)
            swapped = pltpu.roll(placed, half, 1)
            right_re[record, start : start + block, :] = jnp.where(low, placed, swapped)
            right_im[record, start : start + block, :] = jnp.where(low, swapped, placed)
    mine = lax.axis_index("col")
    scale = 1.0 / records
    copies = []
    for step in range(ncols):
        piece = lefts[step][...].astype(jnp.float32) * scale
        swapped = pltpu.roll(piece, half, 1)
        left_turned[...] = jnp.where(low, swapped, -swapped)
        left[...] = piece

        @pl.loop(0, count // TILE)
        def _(j):
            rows = pl.ds(pl.multiple_of(j * TILE, TILE), TILE)
            res = [right_re[e, rows, :] for e in range(records)]
            ims = [right_im[e, rows, :] for e in range(records)]
            for k in range(CH_DEV):
                total = None
                for e in range(records):
                    a = left[k * records + e : k * records + e + 1, :]
                    b = left_turned[k * records + e : k * records + e + 1, :]
                    term = a * res[e] + b * ims[e]
                    total = term if total is None else total + term
                tiles[step, k, rows, :] = total.astype(tiles.dtype)

        place = lax.rem(mine - step + ncols, ncols)
        copies.append(
            pltpu.make_async_copy(tiles.at[step], out.at[pl.ds(place * CH_DEV, CH_DEV)], sems.at[step])
        )
        copies[-1].start()
    for copy in copies:
        copy.wait()


def stacked(packets, lefts, records):
    nrows, ncols = len(packets), len(lefts)
    width = packets[0].shape[1]
    count = nrows * CH_DEV
    vmem = pl.BlockSpec(memory_space=pltpu.VMEM)
    return pl.pallas_call(
        functools.partial(stack_kernel, records, nrows, ncols),
        out_shape=jax.ShapeDtypeStruct((ncols * CH_DEV, count, width), jnp.bfloat16),
        in_specs=[vmem] * (nrows + ncols),
        out_specs=pl.BlockSpec(memory_space=pl.ANY),
        scratch_shapes=[
            pltpu.VMEM((records, count, width), jnp.float32),
            pltpu.VMEM((records, count, width), jnp.float32),
            pltpu.VMEM((CH_DEV * records, width), jnp.float32),
            pltpu.VMEM((CH_DEV * records, width), jnp.float32),
            pltpu.VMEM((ncols, CH_DEV, count, width), jnp.bfloat16),
            pltpu.SemaphoreType.DMA((ncols,)),
        ],
        name="stack",
    )(*packets, *lefts)


def shifted(block, axis):
    size = lax.axis_size(axis)
    return [block] + [
        lax.ppermute(block, axis, [(i, (i + s) % size) for i in range(size)]) for s in range(1, size)
    ]


def on_device(raw_files, file_channels, reader_counts, fir_taps, band_bins):
    ncols = lax.axis_size("col")
    records = raw_files.shape[2]
    packet = whiten(raw_files, file_channels, reader_counts, fir_taps, band_bins, ncols)
    packets = shifted(packet, "row")
    own = own_block(packets, records)
    lefts = shifted(own, "col")
    return stacked(packets, lefts, records)[:, None, :, :]


def solution(mesh):
    return jax.shard_map(
        on_device,
        mesh=mesh,
        in_specs=(
            P(("groups", "row"), "col", None, None),
            P(("groups", "row"), "col"),
            P(("groups", "row"), "col"),
            P(),
            P(),
        ),
        out_specs=P(("groups", "row"), "col", None, None),
        check_vma=False,
    )
```

```python
import functools
import math

import jax
import jax.numpy as jnp
from jax import lax
from jax.experimental import pallas as pl
from jax.experimental.pallas import tpu as pltpu
from jax.sharding import PartitionSpec as P

CH_DEV = 16
DEC = 4
SPAN = 512
LANES = 128
TILE = 16
CHUNK = 64
BEHIND = 4
MXU = 256
SMALL = 16 << 20
ROW_ORDER = (1, 2, 3)
COL_ORDER = (1, 2, 3)
SIN = (6.283185307, -41.341702147, 81.60523051, -76.704495669, 42.014104466, -14.423992009)


def split(x):
    high = x.astype(jnp.bfloat16)
    return high, (x - high.astype(jnp.float32)).astype(jnp.bfloat16)


def turn_cos(steps, length):
    steps = steps - jnp.round(steps * (1.0 / length)) * length
    gap = 0.25 - jnp.abs(steps * (1.0 / length))
    square = gap * gap
    value = jnp.full_like(gap, SIN[-1])
    for term in SIN[-2::-1]:
        value = value * square + term
    return value * gap


def dot(a, b):
    return jnp.dot(a, b, preferred_element_type=jnp.float32)


def dot_t(a, b):
    return lax.dot_general(a, b, (((1,), (1,)), ((), ())), preferred_element_type=jnp.float32)


def iota(shape, axis):
    return lax.broadcasted_iota(jnp.int32, shape, axis)


def whiten_kernel(ncols, records, counts, raw, taps_in, bins_in, channels_in, out, held, taps, bins, channels, sems):
    rows, samples = raw.shape
    taps_count = taps.shape[1]
    length = samples // DEC
    chunks = rows // CHUNK
    small = []
    for index, (source, target) in enumerate(((taps_in, taps), (bins_in, bins), (channels_in, channels))):
        small.append(pltpu.make_async_copy(source, target, sems.at[chunks + index]))
        small[-1].start()
    copies = []
    for index in range(chunks):
        part = pl.ds(index * CHUNK, CHUNK)
        copies.append(pltpu.make_async_copy(raw.at[part, :], held.at[part, :], sems.at[index]))
        copies[-1].start()
    for copy in small:
        copy.wait()
    width = out.shape[1]
    half = width // 2
    before = taps_count // DEC - 1
    reach = LANES // DEC + before
    depth = (reach + TILE - 1) // TILE * TILE
    base = bins[...].astype(jnp.float32)
    band = jnp.concatenate([base, base], axis=1)
    eye = iota((width, width), 0) == iota((width, width), 1)
    band_col = jnp.sum(jnp.where(eye, band, 0.0), axis=1, keepdims=True)
    upper = iota((width, 1), 0) < half
    quarter = 0.25 * length
    place = iota((width, LANES), 1)
    extra = place - reach
    steps = jnp.where(place < reach, place - before, (extra // 2 + 1) * (LANES // DEC))
    shift = jnp.where(place < reach, iota((width, LANES), 0) // half, extra % 2)
    angles = band_col * steps.astype(jnp.float32) - shift.astype(jnp.float32) * quarter
    values = turn_cos(angles, length)
    wave = jnp.where(place < reach, values, 0.0)
    gap = iota((depth, LANES), 1) - DEC * (iota((depth, LANES), 0) - before)
    lane_taps = jnp.concatenate([taps[...], jnp.zeros((1, LANES - taps_count), jnp.float32)], axis=1)
    lane_taps = jnp.broadcast_to(lane_taps, (depth, LANES))
    banded = jnp.take_along_axis(lane_taps, jnp.clip(gap, 0, taps_count - 1), axis=1)
    band_high, band_low = split(jnp.where((gap >= 0) & (gap < taps_count), banded, 0.0))

    nothing = jnp.zeros((depth, LANES), jnp.bfloat16)
    gap_rows = jnp.zeros((LANES - depth, 2 * LANES), jnp.bfloat16)
    taps_rhs = jnp.concatenate(
        [
            jnp.concatenate([band_high, band_low], axis=1),
            gap_rows,
            jnp.concatenate([band_high, nothing], axis=1),
            gap_rows,
        ],
        axis=0,
    )
    waves = jnp.concatenate([wave, jnp.where(place < before, -wave, 0.0)], axis=0)
    waves = jnp.concatenate(split(waves), axis=1)

    def product(acc):
        pltpu.matmul_push_rhs(taps_rhs, 0, 0)
        pltpu.matmul_acc_lhs(acc, waves, load_staged_rhs=0)
        both = pltpu.matmul_pop(acc)
        return both[:, :LANES] + both[:, LANES:]

    filtered = pl.run_scoped(product, pltpu.ACC(0)((2 * width, MXU), jnp.float32))
    first, edge = filtered[:width], filtered[width:]
    swapped = jnp.concatenate([first[half:], first[:half]], axis=0)
    pieces = [first]
    for index in range(SPAN // LANES - 1):
        lane = reach + 2 * index
        cosine, sine = values[:, lane : lane + 1], values[:, lane + 1 : lane + 2]
        pieces.append(first * cosine + swapped * jnp.where(upper, -sine, sine))
    table = jnp.concatenate(split(jnp.concatenate(pieces, axis=1)), axis=0)
    edge = jnp.concatenate(split(edge), axis=0)
    edge = jnp.concatenate([edge, jnp.zeros((2 * width, MXU - LANES), jnp.bfloat16)], axis=1)
    blocks = (samples + SPAN - 1) // SPAN
    turns = (iota((blocks, width), 0) * (SPAN // DEC)).astype(jnp.float32) * band
    cosine = turn_cos(turns, length)
    sine = turn_cos(turns - quarter, length)
    sign = jnp.where(iota((1, width), 1) < half, 1.0, -1.0)
    slots = rows // records
    half_tables = [table[:, index * MXU : (index + 1) * MXU] for index in range(SPAN // MXU)]

    def piece(part, start):
        size = min(MXU, samples - start)
        block = held[part, start : start + size]
        if size < MXU:
            block = jnp.concatenate([block, jnp.zeros((CHUNK, MXU - size), block.dtype)], axis=1)
        return block

    per_unit = (blocks + 1) // 2
    accs = [pltpu.ACC(block % 2)((CHUNK, 2 * width), jnp.float32) for block in range(blocks)]

    def finish(index, along, across):
        spectra = along * sign - pltpu.roll(across, half, 1)
        power = jnp.mean(spectra * spectra, axis=1, keepdims=True)
        white = spectra / jnp.sqrt(power + 1e-06)
        slot = (iota((CHUNK, 1), 0) + index * CHUNK) // records
        out[index * CHUNK : (index + 1) * CHUNK, :] = jnp.where(slot < counts[0, 0], white, 0.0).astype(out.dtype)

    def every_chunk(*accs):
        along = across = None

        def pop(block, along, across):
            both = pltpu.matmul_pop(accs[block])
            term = both[:, :width] + both[:, width:]
            if block == 0:
                return term, jnp.zeros_like(term)
            return along + term * cosine[block : block + 1], across + term * sine[block : block + 1]

        for index in range(chunks):
            copies[index].wait()
            part = pl.ds(index * CHUNK, CHUNK)
            popped = 0
            for step in range(SPAN // MXU):
                for unit in range(2):
                    pltpu.matmul_push_rhs(half_tables[step], step, unit, transpose=True)
                fresh = [step, step]
                for block in range(blocks):
                    if step == 0 and index > 0:
                        along, across = pop(block, along, across)
                    start = block * SPAN + step * MXU
                    if start < samples:
                        if start == 0:
                            pltpu.matmul_push_rhs(edge, 1, 0, transpose=True)
                            pltpu.matmul_acc_lhs(accs[0], piece(part, 0), load_staged_rhs=1)
                        pltpu.matmul_acc_lhs(accs[block], piece(part, start), load_staged_rhs=fresh[block % 2])
                        fresh[block % 2] = None
                    if step == SPAN // MXU - 1 and index == chunks - 1 and block >= BEHIND:
                        along, across = pop(popped, along, across)
                        popped += 1
                if step == 0 and index > 0:
                    finish(index - 1, along, across)
                    along = across = None
        for block in range(popped, blocks):
            along, across = pop(block, along, across)
        finish(chunks - 1, along, across)

    pl.run_scoped(every_chunk, *accs)
    owner = channels[...] // (CH_DEV * ncols)
    local = owner * CH_DEV + channels[...] % CH_DEV
    local = jnp.where(iota((1, slots), 1) < counts[0, 0], local, -1).astype(jnp.float32)
    local = jnp.broadcast_to(
        jnp.concatenate([local, jnp.zeros((1, LANES - slots), jnp.float32)], axis=1), (TILE, LANES)
    )
    source = iota((TILE, LANES), 0) * (LANES // records) + iota((TILE, LANES), 1) // records
    labels = jnp.take_along_axis(local, jnp.minimum(source, slots - 1), axis=1)
    out[rows:, :] = labels.astype(out.dtype)


def whiten(raw_files, file_channels, reader_counts, fir_taps, band_bins, ncols):
    slots, _, records, samples = raw_files.shape
    rows = slots * records
    bins = band_bins.shape[0]
    taps = fir_taps.shape[0]
    width = 2 * bins
    anywhere = pl.BlockSpec(memory_space=pl.ANY)
    return pl.pallas_call(
        functools.partial(whiten_kernel, ncols, records),
        out_shape=jax.ShapeDtypeStruct((rows + TILE, width), jnp.bfloat16),
        in_specs=[pl.BlockSpec(memory_space=pltpu.SMEM), pl.BlockSpec(memory_space=pltpu.HBM)] + [anywhere] * 3,
        out_specs=pl.BlockSpec(memory_space=pltpu.VMEM),
        scratch_shapes=[
            pltpu.VMEM((rows, samples), jnp.bfloat16),
            pltpu.VMEM((1, taps), jnp.float32),
            pltpu.VMEM((1, bins), jnp.int32),
            pltpu.VMEM((1, slots), jnp.int32),
            pltpu.SemaphoreType.DMA((rows // CHUNK + 3,)),
        ],
        compiler_params=pltpu.CompilerParams(vmem_limit_bytes=SMALL),
        cost_estimate=pl.CostEstimate(
            flops=4 * rows * samples * width, bytes_accessed=2 * rows * samples, transcendentals=0
        ),
        name="whiten",
    )(
        reader_counts,
        raw_files.reshape(rows, samples),
        fir_taps.reshape(1, -1),
        band_bins.reshape(1, -1),
        file_channels.reshape(1, -1),
    )


def placing(packet, targets, records):
    rows = packet.shape[0] - TILE
    picks = []
    for group in range(rows // LANES):
        labels = packet[rows : rows + TILE, :].astype(jnp.float32)[group : group + 1]
        keys = labels * records + (iota((1, LANES), 1) % records).astype(jnp.float32)
        picks.append((targets == keys).astype(jnp.float32).astype(jnp.bfloat16))
    return jnp.concatenate(picks, axis=1)


def gather_rows(packets, targets, records):
    picks = jnp.concatenate([placing(p, targets, records) for p in packets], axis=1)
    data = jnp.concatenate([p[: p.shape[0] - TILE, :] for p in packets], axis=0)
    return dot(picks, data)


def own_kernel(records, *refs):
    packets, out = refs[:-1], refs[-1]
    count = out.shape[0]
    first = lax.axis_index("row") * count
    targets = (iota((count, 1), 0) + first).astype(jnp.float32)
    out[...] = gather_rows(packets, targets, records).astype(out.dtype)


def own_block(packets, records):
    vmem = pl.BlockSpec(memory_space=pltpu.VMEM)
    return pl.pallas_call(
        functools.partial(own_kernel, records),
        out_shape=jax.ShapeDtypeStruct((CH_DEV * records, packets[0].shape[1]), packets[0].dtype),
        in_specs=[vmem] * len(packets),
        out_specs=vmem,
        compiler_params=pltpu.CompilerParams(vmem_limit_bytes=SMALL),
        name="own",
    )(*packets)


def stack_piece(records, place, left, right_re, right_im, out, turned, tiles, sem):
    width = left.shape[1]
    half = width // 2
    count = right_re.shape[1]
    low = iota((1, width), 1) < half
    piece = left[...].astype(jnp.float32) * (1.0 / records)
    swapped = pltpu.roll(piece, half, 1)
    turned[0] = piece
    turned[1] = jnp.where(low, swapped, -swapped)

    @pl.loop(0, count // TILE)
    def _(j):
        rows = pl.ds(pl.multiple_of(j * TILE, TILE), TILE)
        res = [right_re[e, rows, :] for e in range(records)]
        ims = [right_im[e, rows, :] for e in range(records)]
        for k in range(CH_DEV):
            total = None
            for e in range(records):
                at = slice(k * records + e, k * records + e + 1)
                term = turned[0, at, :] * res[e] + turned[1, at, :] * ims[e]
                total = term if total is None else total + term
            tiles[k, rows, :] = total.astype(tiles.dtype)

    copy = pltpu.make_async_copy(tiles, out.at[pl.ds(place * CH_DEV, CH_DEV)], sem)
    copy.start()
    copy.wait()


def first_kernel(records, *refs):
    packets = refs[:-7]
    left, out, right_re, right_im, turned, tiles, sem = refs[-7:]
    width = left.shape[1]
    half = width // 2
    count = right_re.shape[1]
    low = iota((1, width), 1) < half
    for start in range(0, count, 64):
        block = min(64, count - start)
        row = iota((block * records, 1), 0)
        targets = ((row % block + start) * records + row // block).astype(jnp.float32)
        placed = gather_rows(packets, targets, records)
        swapped = pltpu.roll(placed, half, 1)
        res = jnp.where(low, placed, swapped)
        ims = jnp.where(low, swapped, placed)
        for record in range(records):
            right_re[record, start : start + block, :] = res[record * block : (record + 1) * block]
            right_im[record, start : start + block, :] = ims[record * block : (record + 1) * block]
    stack_piece(records, lax.axis_index("col"), left, right_re, right_im, out, turned, tiles, sem)


def next_kernel(records, shift, left, right_re, right_im, before, out, turned, tiles, sem):
    place = partner(lax.axis_index("col"), shift, before.shape[0] // CH_DEV, True)
    stack_piece(records, place, left, right_re, right_im, out, turned, tiles, sem)


def stacked(packets, lefts, records):
    nrows, ncols = len(packets), len(lefts)
    width = packets[0].shape[1]
    count = nrows * CH_DEV
    vmem = pl.BlockSpec(memory_space=pltpu.VMEM)
    anywhere = pl.BlockSpec(memory_space=pl.ANY)
    whole = jax.ShapeDtypeStruct((ncols * CH_DEV, count, width), jnp.bfloat16)
    right = jax.ShapeDtypeStruct((records, count, width), jnp.float32)
    scratch = [
        pltpu.VMEM((2, CH_DEV * records, width), jnp.float32),
        pltpu.VMEM((CH_DEV, count, width), jnp.bfloat16),
        pltpu.SemaphoreType.DMA,
    ]
    params = pltpu.CompilerParams(vmem_limit_bytes=SMALL)
    work = 4 * CH_DEV * count * width * records
    cost = pl.CostEstimate(flops=256 * work, bytes_accessed=whole.size * 2 // ncols, transcendentals=0)
    out, right_re, right_im = pl.pallas_call(
        functools.partial(first_kernel, records),
        out_shape=(whole, right, right),
        in_specs=[vmem] * (nrows + 1),
        out_specs=(anywhere, vmem, vmem),
        scratch_shapes=scratch,
        compiler_params=params,
        cost_estimate=cost,
        name="first",
    )(*packets, lefts[0][1])
    for shift, left in lefts[1:]:
        out = pl.pallas_call(
            functools.partial(next_kernel, records, shift),
            out_shape=whole,
            in_specs=[vmem] * 3 + [anywhere],
            out_specs=anywhere,
            scratch_shapes=scratch,
            input_output_aliases={3: 0},
            compiler_params=params,
            cost_estimate=cost,
            name="next",
        )(left, right_re, right_im, out)
    return out


def partner(index, shift, size, back=False):
    if size & (size - 1) == 0:
        return index ^ shift
    return (index + (size - shift if back else shift)) % size


def shifted(block, axis, order):
    size = lax.axis_size(axis)
    shifts = list(order) if len(order) == size - 1 else list(range(1, size))
    return [(0, block)] + [
        (s, lax.ppermute(block, axis, [(i, partner(i, s, size)) for i in range(size)])) for s in shifts
    ]


def on_device(raw_files, file_channels, reader_counts, fir_taps, band_bins):
    ncols = lax.axis_size("col")
    records = raw_files.shape[2]
    packet = whiten(raw_files, file_channels, reader_counts, fir_taps, band_bins, ncols)
    packets = [block for _, block in shifted(packet, "row", ROW_ORDER)]
    own = own_block(packets, records)
    lefts = shifted(own, "col", COL_ORDER)
    return stacked(packets, lefts, records)[:, None, :, :]


def solution(mesh):
    return jax.shard_map(
        on_device,
        mesh=mesh,
        in_specs=(
            P(("groups", "row"), "col", None, None),
            P(("groups", "row"), "col"),
            P(("groups", "row"), "col"),
            P(),
            P(),
        ),
        out_specs=P(("groups", "row"), "col", None, None),
        check_vma=False,
    )
```

```python
import functools
import math

import jax
import jax.numpy as jnp
from jax import lax
from jax.experimental import pallas as pl
from jax.experimental.pallas import tpu as pltpu
from jax.sharding import PartitionSpec as P

CH_DEV = 16
DEC = 4
SPAN = 512
LANES = 128
TILE = 16
CHUNK = 64
BEHIND = 4
MXU = 256
SMALL = 16 << 20
ROW_ORDER = (1, 2, 3)
COL_ORDER = (1, 2, 3)
SIN = (6.283185307, -41.341702147, 81.60523051, -76.704495669, 42.014104466, -14.423992009)


def split(x):
    high = x.astype(jnp.bfloat16)
    return high, (x - high.astype(jnp.float32)).astype(jnp.bfloat16)


def turn_cos(steps, length):
    steps = steps - jnp.round(steps * (1.0 / length)) * length
    gap = 0.25 - jnp.abs(steps * (1.0 / length))
    square = gap * gap
    value = jnp.full_like(gap, SIN[-1])
    for term in SIN[-2::-1]:
        value = value * square + term
    return value * gap


def dot(a, b):
    return jnp.dot(a, b, preferred_element_type=jnp.float32)


def dot_t(a, b):
    return lax.dot_general(a, b, (((1,), (1,)), ((), ())), preferred_element_type=jnp.float32)


def iota(shape, axis):
    return lax.broadcasted_iota(jnp.int32, shape, axis)


def whiten_kernel(ncols, records, *refs):
    (raw, taps_in, bins_in, channels_in), counts, refs = refs[:4], refs[4:-6], refs[-6:]
    out, held, taps, bins, channels, sems = refs
    rows, samples = raw.shape
    taps_count = taps.shape[1]
    length = samples // DEC
    chunks = rows // CHUNK
    small = []
    for index, (source, target) in enumerate(((taps_in, taps), (bins_in, bins), (channels_in, channels))):
        small.append(pltpu.make_async_copy(source, target, sems.at[chunks + index]))
        small[-1].start()
    copies = []
    for index in range(chunks):
        part = pl.ds(index * CHUNK, CHUNK)
        copies.append(pltpu.make_async_copy(raw.at[part, :], held.at[part, :], sems.at[index]))
        copies[-1].start()
    for copy in small:
        copy.wait()
    width = out.shape[1]
    half = width // 2
    before = taps_count // DEC - 1
    reach = LANES // DEC + before
    depth = (reach + TILE - 1) // TILE * TILE
    base = bins[...].astype(jnp.float32)
    band = jnp.concatenate([base, base], axis=1)
    eye = iota((width, width), 0) == iota((width, width), 1)
    band_col = jnp.sum(jnp.where(eye, band, 0.0), axis=1, keepdims=True)
    upper = iota((width, 1), 0) < half
    quarter = 0.25 * length
    place = iota((width, LANES), 1)
    extra = place - reach
    steps = jnp.where(place < reach, place - before, (extra // 2 + 1) * (LANES // DEC))
    shift = jnp.where(place < reach, iota((width, LANES), 0) // half, extra % 2)
    angles = band_col * steps.astype(jnp.float32) - shift.astype(jnp.float32) * quarter
    values = turn_cos(angles, length)
    wave = jnp.where(place < reach, values, 0.0)
    gap = iota((depth, LANES), 1) - DEC * (iota((depth, LANES), 0) - before)
    lane_taps = jnp.concatenate([taps[...], jnp.zeros((1, LANES - taps_count), jnp.float32)], axis=1)
    lane_taps = jnp.broadcast_to(lane_taps, (depth, LANES))
    banded = jnp.take_along_axis(lane_taps, jnp.clip(gap, 0, taps_count - 1), axis=1)
    band_high, band_low = split(jnp.where((gap >= 0) & (gap < taps_count), banded, 0.0))

    nothing = jnp.zeros((depth, LANES), jnp.bfloat16)
    gap_rows = jnp.zeros((LANES - depth, 2 * LANES), jnp.bfloat16)
    taps_rhs = jnp.concatenate(
        [
            jnp.concatenate([band_high, band_low], axis=1),
            gap_rows,
            jnp.concatenate([band_high, nothing], axis=1),
            gap_rows,
        ],
        axis=0,
    )
    waves = jnp.concatenate([wave, jnp.where(place < before, -wave, 0.0)], axis=0)
    waves = jnp.concatenate(split(waves), axis=1)

    def product(acc):
        pltpu.matmul_push_rhs(taps_rhs, 0, 0)
        pltpu.matmul_acc_lhs(acc, waves, load_staged_rhs=0)
        both = pltpu.matmul_pop(acc)
        return both[:, :LANES] + both[:, LANES:]

    filtered = pl.run_scoped(product, pltpu.ACC(0)((2 * width, MXU), jnp.float32))
    first, edge = filtered[:width], filtered[width:]
    swapped = jnp.concatenate([first[half:], first[:half]], axis=0)
    pieces = [first]
    for index in range(SPAN // LANES - 1):
        lane = reach + 2 * index
        cosine, sine = values[:, lane : lane + 1], values[:, lane + 1 : lane + 2]
        pieces.append(first * cosine + swapped * jnp.where(upper, -sine, sine))
    table = jnp.concatenate(split(jnp.concatenate(pieces, axis=1)), axis=0)
    edge = jnp.concatenate(split(edge), axis=0)
    edge = jnp.concatenate([edge, jnp.zeros((2 * width, MXU - LANES), jnp.bfloat16)], axis=1)
    blocks = (samples + SPAN - 1) // SPAN
    turns = (iota((blocks, width), 0) * (SPAN // DEC)).astype(jnp.float32) * band
    cosine = turn_cos(turns, length)
    sine = turn_cos(turns - quarter, length)
    sign = jnp.where(iota((1, width), 1) < half, 1.0, -1.0)
    slots = rows // records
    half_tables = [table[:, index * MXU : (index + 1) * MXU] for index in range(SPAN // MXU)]

    def piece(part, start):
        size = min(MXU, samples - start)
        block = held[part, start : start + size]
        if size < MXU:
            block = jnp.concatenate([block, jnp.zeros((CHUNK, MXU - size), block.dtype)], axis=1)
        return block

    per_unit = (blocks + 1) // 2
    accs = [pltpu.ACC(block % 2)((CHUNK, 2 * width), jnp.float32) for block in range(blocks)]

    def finish(index, along, across):
        spectra = along * sign - pltpu.roll(across, half, 1)
        power = jnp.mean(spectra * spectra, axis=1, keepdims=True)
        white = spectra / jnp.sqrt(power + 1e-06)
        if counts:
            slot = (iota((CHUNK, 1), 0) + index * CHUNK) // records
            white = jnp.where(slot < counts[0][0, 0], white, 0.0)
        out[index * CHUNK : (index + 1) * CHUNK, :] = white.astype(out.dtype)

    def every_chunk(*accs):
        along = across = None

        def pop(block, along, across):
            both = pltpu.matmul_pop(accs[block])
            term = both[:, :width] + both[:, width:]
            if block == 0:
                return term, jnp.zeros_like(term)
            return along + term * cosine[block : block + 1], across + term * sine[block : block + 1]

        for index in range(chunks):
            copies[index].wait()
            part = pl.ds(index * CHUNK, CHUNK)
            popped = 0
            for step in range(SPAN // MXU):
                for unit in range(2):
                    pltpu.matmul_push_rhs(half_tables[step], step, unit, transpose=True)
                fresh = [step, step]
                for block in range(blocks):
                    if step == 0 and index > 0:
                        along, across = pop(block, along, across)
                    start = block * SPAN + step * MXU
                    if start < samples:
                        if start == 0:
                            pltpu.matmul_push_rhs(edge, 1, 0, transpose=True)
                            pltpu.matmul_acc_lhs(accs[0], piece(part, 0), load_staged_rhs=1)
                        pltpu.matmul_acc_lhs(accs[block], piece(part, start), load_staged_rhs=fresh[block % 2])
                        fresh[block % 2] = None
                    if step == SPAN // MXU - 1 and index == chunks - 1 and block >= BEHIND:
                        along, across = pop(popped, along, across)
                        popped += 1
                if step == 0 and index > 0:
                    finish(index - 1, along, across)
                    along = across = None
        for block in range(popped, blocks):
            along, across = pop(block, along, across)
        finish(chunks - 1, along, across)

    pl.run_scoped(every_chunk, *accs)
    owner = channels[...] // (CH_DEV * ncols)
    local = owner * CH_DEV + channels[...] % CH_DEV
    if counts:
        local = jnp.where(iota((1, slots), 1) < counts[0][0, 0], local, -1)
    local = local.astype(jnp.float32)
    local = jnp.broadcast_to(
        jnp.concatenate([local, jnp.zeros((1, LANES - slots), jnp.float32)], axis=1), (TILE, LANES)
    )
    source = iota((TILE, LANES), 0) * (LANES // records) + iota((TILE, LANES), 1) // records
    labels = jnp.take_along_axis(local, jnp.minimum(source, slots - 1), axis=1)
    out[rows:, :] = labels.astype(out.dtype)


def whiten(raw_files, file_channels, reader_counts, fir_taps, band_bins, ncols):
    slots, _, records, samples = raw_files.shape
    rows = slots * records
    bins = band_bins.shape[0]
    taps = fir_taps.shape[0]
    width = 2 * bins
    counts = [] if slots == CH_DEV else [reader_counts]
    anywhere = pl.BlockSpec(memory_space=pl.ANY)
    return pl.pallas_call(
        functools.partial(whiten_kernel, ncols, records),
        out_shape=jax.ShapeDtypeStruct((rows + TILE, width), jnp.bfloat16),
        in_specs=[anywhere] * 4 + [pl.BlockSpec(memory_space=pltpu.SMEM)] * len(counts),
        out_specs=pl.BlockSpec(memory_space=pltpu.VMEM),
        scratch_shapes=[
            pltpu.VMEM((rows, samples), jnp.bfloat16),
            pltpu.VMEM((1, taps), jnp.float32),
            pltpu.VMEM((1, bins), jnp.int32),
            pltpu.VMEM((1, slots), jnp.int32),
            pltpu.SemaphoreType.DMA((rows // CHUNK + 3,)),
        ],
        compiler_params=pltpu.CompilerParams(vmem_limit_bytes=SMALL),
        cost_estimate=pl.CostEstimate(
            flops=4 * rows * samples * width, bytes_accessed=2 * rows * samples, transcendentals=0
        ),
        name="whiten",
    )(
        *(
            pltpu.with_memory_space_constraint(x, pltpu.HBM)
            for x in (
                raw_files.reshape(rows, samples),
                fir_taps.reshape(1, -1),
                band_bins.reshape(1, -1),
                file_channels.reshape(1, -1),
            )
        ),
        *counts,
    )


def placing(packet, targets, records):
    rows = packet.shape[0] - TILE
    picks = []
    for group in range(rows // LANES):
        labels = packet[rows : rows + TILE, :].astype(jnp.float32)[group : group + 1]
        keys = labels * records + (iota((1, LANES), 1) % records).astype(jnp.float32)
        picks.append((targets == keys).astype(jnp.float32).astype(jnp.bfloat16))
    return jnp.concatenate(picks, axis=1)


def gather_rows(packets, targets, records):
    picks = jnp.concatenate([placing(p, targets, records) for p in packets], axis=1)
    data = jnp.concatenate([p[: p.shape[0] - TILE, :] for p in packets], axis=0)
    return dot(picks, data)


def own_kernel(records, *refs):
    packets, out = refs[:-1], refs[-1]
    count = out.shape[0]
    first = lax.axis_index("row") * count
    targets = (iota((count, 1), 0) + first).astype(jnp.float32)
    out[...] = gather_rows(packets, targets, records).astype(out.dtype)


def own_block(packets, records):
    vmem = pl.BlockSpec(memory_space=pltpu.VMEM)
    return pl.pallas_call(
        functools.partial(own_kernel, records),
        out_shape=jax.ShapeDtypeStruct((CH_DEV * records, packets[0].shape[1]), packets[0].dtype),
        in_specs=[vmem] * len(packets),
        out_specs=vmem,
        compiler_params=pltpu.CompilerParams(vmem_limit_bytes=SMALL),
        name="own",
    )(*packets)


def stack_pieces(records, places, lefts, right_re, right_im, out, turned, tiles, sems):
    width = lefts[0].shape[1]
    half = width // 2
    count = right_re.shape[1]
    low = iota((1, width), 1) < half
    copies = []
    for index, (place, left) in enumerate(zip(places, lefts)):
        piece = left[...].astype(jnp.float32) * (1.0 / records)
        swapped = pltpu.roll(piece, half, 1)
        turned[index, 0] = piece
        turned[index, 1] = jnp.where(low, swapped, -swapped)

        @pl.loop(0, count // TILE)
        def _(j):
            rows = pl.ds(pl.multiple_of(j * TILE, TILE), TILE)
            res = [right_re[e, rows, :] for e in range(records)]
            ims = [right_im[e, rows, :] for e in range(records)]
            for k in range(CH_DEV):
                total = None
                for e in range(records):
                    at = slice(k * records + e, k * records + e + 1)
                    term = turned[index, 0, at, :] * res[e] + turned[index, 1, at, :] * ims[e]
                    total = term if total is None else total + term
                tiles[index, k, rows, :] = total.astype(tiles.dtype)

        target = out.at[pl.ds(place * CH_DEV, CH_DEV)]
        copies.append(pltpu.make_async_copy(tiles.at[index], target, sems.at[index]))
        copies[-1].start()
    for copy in copies:
        copy.wait()


def first_kernel(records, *refs):
    packets = refs[:-7]
    left, out, right_re, right_im, turned, tiles, sems = refs[-7:]
    width = left.shape[1]
    half = width // 2
    count = right_re.shape[1]
    low = iota((1, width), 1) < half
    for start in range(0, count, 64):
        block = min(64, count - start)
        row = iota((block * records, 1), 0)
        targets = ((row % block + start) * records + row // block).astype(jnp.float32)
        placed = gather_rows(packets, targets, records)
        swapped = pltpu.roll(placed, half, 1)
        res = jnp.where(low, placed, swapped)
        ims = jnp.where(low, swapped, placed)
        for record in range(records):
            right_re[record, start : start + block, :] = res[record * block : (record + 1) * block]
            right_im[record, start : start + block, :] = ims[record * block : (record + 1) * block]
    stack_pieces(records, [lax.axis_index("col")], [left], right_re, right_im, out, turned, tiles, sems)


def rest_kernel(records, shifts, *refs):
    lefts = refs[: len(shifts)]
    right_re, right_im, before, out, turned, tiles, sems = refs[len(shifts) :]
    mine = lax.axis_index("col")
    places = [partner(mine, shift, before.shape[0] // CH_DEV, True) for shift in shifts]
    stack_pieces(records, places, lefts, right_re, right_im, out, turned, tiles, sems)


def stacked(packets, lefts, records):
    nrows, ncols = len(packets), len(lefts)
    width = packets[0].shape[1]
    count = nrows * CH_DEV
    vmem = pl.BlockSpec(memory_space=pltpu.VMEM)
    anywhere = pl.BlockSpec(memory_space=pl.ANY)
    whole = jax.ShapeDtypeStruct((ncols * CH_DEV, count, width), jnp.bfloat16)
    right = jax.ShapeDtypeStruct((records, count, width), jnp.float32)
    params = pltpu.CompilerParams(vmem_limit_bytes=SMALL)

    def scratch(pieces):
        return [
            pltpu.VMEM((pieces, 2, CH_DEV * records, width), jnp.float32),
            pltpu.VMEM((pieces, CH_DEV, count, width), jnp.bfloat16),
            pltpu.SemaphoreType.DMA((pieces,)),
        ]

    def cost(pieces):
        work = 4 * CH_DEV * count * width * records * pieces
        return pl.CostEstimate(
            flops=256 * work, bytes_accessed=whole.size * 2 * pieces // ncols, transcendentals=0
        )

    out, right_re, right_im = pl.pallas_call(
        functools.partial(first_kernel, records),
        out_shape=(whole, right, right),
        in_specs=[vmem] * (nrows + 1),
        out_specs=(anywhere, vmem, vmem),
        scratch_shapes=scratch(1),
        compiler_params=params,
        cost_estimate=cost(1),
        name="first",
    )(*packets, lefts[0][1])
    others = lefts[1:]
    return pl.pallas_call(
        functools.partial(rest_kernel, records, [shift for shift, _ in others]),
        out_shape=whole,
        in_specs=[vmem] * (len(others) + 2) + [anywhere],
        out_specs=anywhere,
        scratch_shapes=scratch(len(others)),
        input_output_aliases={len(others) + 2: 0},
        compiler_params=params,
        cost_estimate=cost(len(others)),
        name="rest",
    )(*[left for _, left in others], right_re, right_im, out)


def partner(index, shift, size, back=False):
    if size & (size - 1) == 0:
        return index ^ shift
    return (index + (size - shift if back else shift)) % size


def shifted(block, axis, order):
    size = lax.axis_size(axis)
    shifts = list(order) if len(order) == size - 1 else list(range(1, size))
    return [(0, block)] + [
        (s, lax.ppermute(block, axis, [(i, partner(i, s, size)) for i in range(size)])) for s in shifts
    ]


def on_device(raw_files, file_channels, reader_counts, fir_taps, band_bins):
    ncols = lax.axis_size("col")
    records = raw_files.shape[2]
    packet = whiten(raw_files, file_channels, reader_counts, fir_taps, band_bins, ncols)
    packets = [block for _, block in shifted(packet, "row", ROW_ORDER)]
    own = own_block(packets, records)
    lefts = shifted(own, "col", COL_ORDER)
    return stacked(packets, lefts, records)[:, None, :, :]


def solution(mesh):
    return jax.shard_map(
        on_device,
        mesh=mesh,
        in_specs=(
            P(("groups", "row"), "col", None, None),
            P(("groups", "row"), "col"),
            P(("groups", "row"), "col"),
            P(),
            P(),
        ),
        out_specs=P(("groups", "row"), "col", None, None),
        check_vma=False,
    )
```

```python
import functools
import math

import jax
import jax.numpy as jnp
from jax import lax
from jax.experimental import pallas as pl
from jax.experimental.pallas import tpu as pltpu
from jax.sharding import PartitionSpec as P

CH_DEV = 16
DEC = 4
SPAN = 1024
LANES = 128
TILE = 16
BLOCK = 64
EARLY = 1
CHAINS = 2
GROUP = 128
HALF = 64
CUTS = (4, 8)
MXU = 256
SMALL = 16 << 20
ROW_ORDER = (1, 2, 3)
COL_ORDER = (1, 2, 3)
USE_ORDER = (1, 2, 3)
SIN = (6.283185307, -41.341702147, 81.60523051, -76.704495669, 42.014104466, -14.423992009)


def split(x):
    high = x.astype(jnp.bfloat16)
    return high, (x - high.astype(jnp.float32)).astype(jnp.bfloat16)


def turn_cos(steps, length):
    steps = steps - jnp.round(steps * (1.0 / length)) * length
    gap = 0.25 - jnp.abs(steps * (1.0 / length))
    square = gap * gap
    value = jnp.full_like(gap, SIN[-1])
    for term in SIN[-2::-1]:
        value = value * square + term
    return value * gap


def dot(a, b):
    return jnp.dot(a, b, preferred_element_type=jnp.float32)


def dot_t(a, b):
    return lax.dot_general(a, b, (((1,), (1,)), ((), ())), preferred_element_type=jnp.float32)


def iota(shape, axis):
    return lax.broadcasted_iota(jnp.int32, shape, axis)


def whiten_kernel(ncols, records, *refs):
    (raw, taps_in, bins_in, channels_in), counts, refs = refs[:4], refs[4:-8], refs[-8:]
    out, held, taps, bins, channels, waves, ordered, sems = refs
    rows, samples = raw.shape
    taps_count = taps.shape[1]
    length = samples // DEC
    blocks = (samples + SPAN - 1) // SPAN
    sets = [range(a, min(b, blocks)) for a, b in zip((0,) + CUTS, CUTS + (blocks,)) if a < blocks]
    small = []
    for index, (source, target) in enumerate(((taps_in, taps), (bins_in, bins), (channels_in, channels))):
        small.append(pltpu.make_async_copy(source, target, sems.at[index]))
        small[-1].start()
    copies = []
    for index, group in enumerate(sets):
        start = group[0] * SPAN
        part = pl.ds(start, min(len(group) * SPAN, samples - start))
        copies.append(pltpu.make_async_copy(raw.at[:, part], held.at[:, part], sems.at[3 + index]))
        copies[-1].start()
    for copy in small:
        copy.wait()
    width = out.shape[1]
    half = width // 2
    before = taps_count // DEC - 1
    tiles = SPAN // LANES
    depth = (LANES // DEC + before + TILE - 1) // TILE * TILE
    quarter = 0.25 * length
    base = bins[...].astype(jnp.float32)
    band = jnp.concatenate([base, base], axis=1)
    turn_at, back_at = depth, depth + tiles
    cos_at = depth + 2 * tiles
    sin_at = cos_at + TILE
    lower = iota((sin_at + TILE, width), 1) // half
    row = iota((sin_at + TILE, width), 0)
    steps = jnp.where(row < turn_at, row - before, (row - turn_at) % tiles * (LANES // DEC))
    steps = jnp.where(row < cos_at, steps, (row - cos_at) % TILE * (SPAN // DEC))
    shift = jnp.where(row < turn_at, lower, 0)
    shift = jnp.where((row >= back_at) & (row < cos_at), 1, shift)
    shift = jnp.where(row >= sin_at, 1, shift)
    values = turn_cos(steps.astype(jnp.float32) * band - shift.astype(jnp.float32) * quarter, length)
    flip = (row >= back_at) & (row < cos_at) & (lower == 0)
    waves[...] = jnp.where(flip, -values, values)
    gap = iota((LANES, LANES), 0) - DEC * (iota((LANES, LANES), 1) - before)
    lane_taps = jnp.concatenate([taps[...], jnp.zeros((1, LANES - taps_count), jnp.float32)], axis=1)
    lane_taps = jnp.broadcast_to(lane_taps, (LANES, LANES))
    banded = jnp.take_along_axis(lane_taps, jnp.clip(gap, 0, taps_count - 1), axis=1)
    banded = jnp.where((gap >= 0) & (gap < taps_count), banded, 0.0)
    edge_rows = (DEC * before + TILE - 1) // TILE * TILE
    early = jnp.where(iota((edge_rows, LANES), 1) < before, -banded[:edge_rows], 0.0)
    filters = jnp.concatenate(split(jnp.concatenate([banded, early], axis=0)), axis=1)
    wave_high, wave_low = split(waves[:depth, :])
    space = jnp.zeros((LANES - depth, 2 * width), jnp.bfloat16)
    rhs = jnp.concatenate(
        [
            jnp.concatenate([wave_high, wave_low], axis=1),
            space,
            jnp.concatenate([wave_high, jnp.zeros_like(wave_low)], axis=1),
            space,
        ],
        axis=0,
    )

    def product(acc):
        pltpu.matmul_push_rhs(rhs, 0, 0)
        pltpu.matmul_acc_lhs(acc, filters, load_staged_rhs=0)
        both = pltpu.matmul_pop(acc)
        return both[:, :width] + both[:, width:]

    filtered = pl.run_scoped(product, pltpu.ACC(0)((LANES + edge_rows, MXU), jnp.float32))
    first, edge = filtered[:LANES], filtered[LANES:]
    swapped = pltpu.roll(first, half, 1)
    half_tables = []
    for index in range(0, tiles, MXU // LANES):
        pieces = []
        for tile in range(index, index + MXU // LANES):
            turned = first * waves[turn_at + tile : turn_at + tile + 1, :]
            turned = turned + swapped * waves[back_at + tile : back_at + tile + 1, :]
            pieces.append(turned if tile else first)
        half_tables.append(jnp.concatenate(split(jnp.concatenate(pieces, axis=0)), axis=1))
    edge = jnp.concatenate(split(edge), axis=1)
    edge = jnp.concatenate([edge, jnp.zeros((MXU - edge_rows, 2 * width), jnp.bfloat16)], axis=0)
    sign = jnp.where(iota((1, width), 1) < half, 1.0, -1.0)
    slots = rows // records

    def piece(part, start):
        size = min(MXU, samples - start)
        block = held[part, start : start + size]
        if size < MXU:
            block = jnp.concatenate([block, jnp.zeros((HALF, MXU - size), block.dtype)], axis=1)
        return block

    accs = [
        pltpu.ACC(block % 2)((HALF, 2 * width), jnp.float32) for block in range(blocks) for _ in range(GROUP // HALF)
    ]

    def finish(top, along, across):
        spectra = along * sign - pltpu.roll(across, half, 1)
        power = jnp.mean(spectra * spectra, axis=1, keepdims=True)
        white = spectra / jnp.sqrt(power + 1e-06)
        if counts:
            slot = (iota((HALF, 1), 0) + top) // records
            white = jnp.where(slot < counts[0][0, 0], white, 0.0)
        for index in range(HALF // records):
            turned = pl.ds(top // records + index, records, stride=slots)
            ordered[turned, :] = white[index * records : (index + 1) * records]

    steps_count = SPAN // MXU

    def used(members, step, unit):
        return [b for b in members if b % 2 == unit and b * SPAN + step * MXU < samples]

    orders = [[step for members in sets for step in range(steps_count) if used(members, step, unit)] for unit in range(2)]

    def push_next(unit, pushed):
        if pushed[unit] < len(orders[unit]):
            pltpu.matmul_push_rhs(half_tables[orders[unit][pushed[unit]]], pushed[unit] % 2, unit)
        pushed[unit] += 1

    def every_group(*accs):
        def pop(block, part, sums):
            both = pltpu.matmul_pop(accs[block * (GROUP // HALF) + part])
            term = both[:, :width] + both[:, width:]
            if block == 0:
                sums[part] = (term, jnp.zeros_like(term))
            else:
                along, across = sums[part]
                along = along + term * waves[cos_at + block : cos_at + block + 1, :]
                across = across + term * waves[sin_at + block : sin_at + block + 1, :]
                sums[part] = (along, across)

        def drain(both, parts, sums):
            for part in range(parts):
                for block in both:
                    pop(block, part, sums)

        for group in range(rows // GROUP):
            tops = [group * GROUP + part * HALF for part in range(GROUP // HALF)]
            sums = [None] * len(tops)
            ready, late = [], []
            pushed = [0, 0]
            pltpu.matmul_push_rhs(edge, 1, 0)
            for unit in range(2):
                push_next(unit, pushed)
            for number, members in enumerate(sets):
                if group == 0:
                    copies[number].wait()
                if number == 0:
                    for part, top in enumerate(tops):
                        lhs = piece(pl.ds(top, HALF), 0)
                        pltpu.matmul_acc_lhs(accs[part], lhs, load_staged_rhs=None if part else 1)
                for step in range(steps_count):
                    fresh = [None, None]
                    for unit in range(2):
                        if used(members, step, unit):
                            fresh[unit] = (pushed[unit] - 1) % 2
                            push_next(unit, pushed)
                    for pair in range(members[0], members[-1] + 1, 2):
                        both = [block for block in (pair, pair + 1) if block in members]
                        for part, top in enumerate(tops):
                            for block in both:
                                start = block * SPAN + step * MXU
                                if start < samples:
                                    acc = accs[block * len(tops) + part]
                                    lhs = piece(pl.ds(top, HALF), start)
                                    pltpu.matmul_acc_lhs(acc, lhs, load_staged_rhs=fresh[block % 2])
                                    fresh[block % 2] = None
                        if ready:
                            drain(ready.pop(0), len(tops), sums)
                        if step == steps_count - 1:
                            late.append(both)
                while ready:
                    drain(ready.pop(0), len(tops), sums)
                ready, late = late, []
            for both in ready:
                drain(both, len(tops), sums)
            for part, top in enumerate(tops):
                finish(top, *sums[part])

    pl.run_scoped(every_group, *accs)
    out[:rows, :] = ordered[...].astype(out.dtype)
    owner = channels[...] // (CH_DEV * ncols)
    local = owner * CH_DEV + channels[...] % CH_DEV
    if counts:
        local = jnp.where(iota((1, slots), 1) < counts[0][0, 0], local, -1)
    local = local.astype(jnp.float32)
    local = jnp.concatenate([local, jnp.zeros((1, LANES - slots), jnp.float32)], axis=1)
    local = jnp.broadcast_to(local, (TILE, LANES))
    labels = jnp.take_along_axis(local, iota((TILE, LANES), 1) % slots, axis=1)
    out[rows:, :] = labels.astype(out.dtype)


def whiten(raw_files, file_channels, reader_counts, fir_taps, band_bins, ncols):
    slots, _, records, samples = raw_files.shape
    rows = slots * records
    bins = band_bins.shape[0]
    taps = fir_taps.shape[0]
    width = 2 * bins
    counts = [] if slots == CH_DEV else [reader_counts]
    anywhere = pl.BlockSpec(memory_space=pl.ANY)
    depth = (LANES // DEC + taps // DEC - 1 + TILE - 1) // TILE * TILE
    table_rows = depth + 2 * (SPAN // LANES) + 2 * TILE
    return pl.pallas_call(
        functools.partial(whiten_kernel, ncols, records),
        out_shape=jax.ShapeDtypeStruct((rows + TILE, width), jnp.bfloat16),
        in_specs=[anywhere] * 4 + [pl.BlockSpec(memory_space=pltpu.SMEM)] * len(counts),
        out_specs=pl.BlockSpec(memory_space=pltpu.VMEM),
        scratch_shapes=[
            pltpu.VMEM((rows, samples), jnp.bfloat16),
            pltpu.VMEM((1, taps), jnp.float32),
            pltpu.VMEM((1, bins), jnp.int32),
            pltpu.VMEM((1, slots), jnp.int32),
            pltpu.VMEM((table_rows, width), jnp.float32),
            pltpu.VMEM((rows, width), jnp.float32),
            pltpu.SemaphoreType.DMA((len(CUTS) + 4,)),
        ],
        compiler_params=pltpu.CompilerParams(vmem_limit_bytes=SMALL),
        cost_estimate=pl.CostEstimate(
            flops=4 * rows * samples * width, bytes_accessed=2 * rows * samples, transcendentals=0
        ),
        name="whiten",
    )(
        *(
            pltpu.with_memory_space_constraint(x, pltpu.HBM)
            for x in (
                raw_files.reshape(rows, samples),
                fir_taps.reshape(1, -1),
                band_bins.reshape(1, -1),
                file_channels.reshape(1, -1),
            )
        ),
        *counts,
    )


def gather_channels(packets, first, count, slots, records):
    held = LANES // slots
    picks = []
    for start in range(0, len(packets), held):
        group = packets[start : start + held]
        lane = iota((1, LANES), 1) // slots
        label = jnp.full((1, LANES), -1.0, jnp.float32)
        for index, packet in enumerate(group):
            row = packet[slots * records : slots * records + TILE, :].astype(jnp.float32)[:1]
            label = jnp.where(lane == index, row, label)
        wanted = (iota((count, 1), 0) + first).astype(jnp.float32)
        pick = (wanted == label).astype(jnp.float32).astype(jnp.bfloat16)
        picks.append(pick[:, : len(group) * slots])
    data = [
        jnp.concatenate([packet[e * slots : (e + 1) * slots, :] for e in range(records)], axis=1)
        for packet in packets
    ]
    return dot(jnp.concatenate(picks, axis=1), jnp.concatenate(data, axis=0))


def own_kernel(records, slots, *refs):
    packets, out = refs[:-1], refs[-1]
    width = out.shape[1]
    placed = gather_channels(packets, lax.axis_index("row") * CH_DEV, CH_DEV, slots, records)
    for e in range(records):
        out[e * CH_DEV : (e + 1) * CH_DEV, :] = placed[:, e * width : (e + 1) * width].astype(out.dtype)


def own_block(packets, records, slots):
    vmem = pl.BlockSpec(memory_space=pltpu.VMEM)
    return pl.pallas_call(
        functools.partial(own_kernel, records, slots),
        out_shape=jax.ShapeDtypeStruct((CH_DEV * records, packets[0].shape[1]), packets[0].dtype),
        in_specs=[vmem] * len(packets),
        out_specs=vmem,
        compiler_params=pltpu.CompilerParams(vmem_limit_bytes=SMALL),
        name="own",
    )(*packets)


def stack_piece(records, left, right_re, right_im, turned, tile):
    width = left.shape[1]
    half = width // 2
    count = right_re.shape[1]
    low = iota((1, width), 1) < half
    piece = left[...].astype(jnp.float32) * (1.0 / records)
    swapped = pltpu.roll(piece, half, 1)
    turned[0] = piece
    turned[1] = jnp.where(low, swapped, -swapped)

    @pl.loop(0, count // BLOCK)
    def _(j):
        rows = pl.ds(pl.multiple_of(j * BLOCK, BLOCK), BLOCK)
        res = [right_re[e, rows, :] for e in range(records)]
        ims = [right_im[e, rows, :] for e in range(records)]
        for k in range(CH_DEV):
            terms = [None] * CHAINS
            for e in range(records):
                at = slice(e * CH_DEV + k, e * CH_DEV + k + 1)
                for side, right in ((0, res[e]), (1, ims[e])):
                    wide = jnp.broadcast_to(turned[side, at, :], (TILE, width)).astype(jnp.bfloat16)
                    term = jnp.concatenate([wide] * (BLOCK // TILE), axis=0) * right
                    chain = (2 * e + side) % CHAINS
                    terms[chain] = term if terms[chain] is None else terms[chain] + term
            while len(terms) > 1:
                terms = [a + b for a, b in zip(terms[::2], terms[1::2])] + terms[len(terms) // 2 * 2 :]
            tile[k, rows, :] = terms[0]


def first_kernel(records, slots, *refs):
    packets = refs[:-5]
    left, tile, right_re, right_im, turned = refs[-5:]
    width = left.shape[1]
    half = width // 2
    count = right_re.shape[1]
    low = iota((1, width), 1) < half
    for start in range(0, count, BLOCK):
        placed = gather_channels(packets, start, BLOCK, slots, records)
        for e in range(records):
            one = placed[:, e * width : (e + 1) * width]
            swapped = pltpu.roll(one, half, 1)
            right_re[e, start : start + BLOCK, :] = jnp.where(low, one, swapped).astype(right_re.dtype)
            right_im[e, start : start + BLOCK, :] = jnp.where(low, swapped, one).astype(right_im.dtype)
    stack_piece(records, left, right_re, right_im, turned, tile)


def next_kernel(records, left, right_re, right_im, tile, turned):
    stack_piece(records, left, right_re, right_im, turned, tile)


def last_kernel(records, shifts, made, *refs):
    done, refs = refs[:made], refs[made:]
    lefts, refs = refs[: len(shifts) - made], refs[len(shifts) - made :]
    right_re, right_im, out, turned, tiles, sems = refs
    mine = lax.axis_index("col")
    copies = []

    def send(tile, index):
        place = partner(mine, shifts[index], len(shifts), True)
        copies.append(pltpu.make_async_copy(tile, out.at[pl.ds(place * CH_DEV, CH_DEV)], sems.at[index]))
        copies[-1].start()

    for index, tile in enumerate(done):
        send(tile, index)
    for index, left in enumerate(lefts):
        stack_piece(records, left, right_re, right_im, turned, tiles.at[index])
        send(tiles.at[index], made + index)
    for copy in copies:
        copy.wait()


def stacked(packets, lefts, records, slots):
    nrows, ncols = len(packets), len(lefts)
    width = packets[0].shape[1]
    count = nrows * CH_DEV
    vmem = pl.BlockSpec(memory_space=pltpu.VMEM)
    right = jax.ShapeDtypeStruct((records, count, width), jnp.bfloat16)
    tile = jax.ShapeDtypeStruct((CH_DEV, count, width), jnp.bfloat16)
    turned = pltpu.VMEM((2, CH_DEV * records, width), jnp.float32)
    params = pltpu.CompilerParams(vmem_limit_bytes=SMALL)

    def cost(pieces):
        work = 4 * CH_DEV * count * width * records * pieces
        return pl.CostEstimate(flops=256 * work, bytes_accessed=tile.size * 2 * pieces, transcendentals=0)

    first, right_re, right_im = pl.pallas_call(
        functools.partial(first_kernel, records, slots),
        out_shape=(tile, right, right),
        in_specs=[vmem] * (nrows + 1),
        out_specs=(vmem,) * 3,
        scratch_shapes=[turned],
        compiler_params=params,
        cost_estimate=cost(1),
        name="first",
    )(*packets, lefts[0][1])
    tiles = [first]
    early = min(EARLY, ncols - 2)
    for _, left in lefts[1 : 1 + early]:
        tiles.append(
            pl.pallas_call(
                functools.partial(next_kernel, records),
                out_shape=tile,
                in_specs=[vmem] * 3,
                out_specs=vmem,
                scratch_shapes=[turned],
                compiler_params=params,
                cost_estimate=cost(1),
                name="next",
            )(left, right_re, right_im)
        )
    others = [left for _, left in lefts[1 + early :]]
    return pl.pallas_call(
        functools.partial(last_kernel, records, [shift for shift, _ in lefts], len(tiles)),
        out_shape=jax.ShapeDtypeStruct((ncols * CH_DEV, count, width), jnp.bfloat16),
        in_specs=[vmem] * (len(tiles) + len(others) + 2),
        out_specs=pl.BlockSpec(memory_space=pl.ANY),
        scratch_shapes=[
            turned,
            pltpu.VMEM((len(others), CH_DEV, count, width), jnp.bfloat16),
            pltpu.SemaphoreType.DMA((ncols,)),
        ],
        compiler_params=params,
        cost_estimate=cost(len(others)),
        name="last",
    )(*tiles, *others, right_re, right_im)


def partner(index, shift, size, back=False):
    if size & (size - 1) == 0:
        return index ^ shift
    return (index + (size - shift if back else shift)) % size


def shifted(block, axis, order):
    size = lax.axis_size(axis)
    shifts = list(order) if len(order) == size - 1 else list(range(1, size))
    return [(0, block)] + [
        (s, lax.ppermute(block, axis, [(i, partner(i, s, size)) for i in range(size)])) for s in shifts
    ]


def on_device(raw_files, file_channels, reader_counts, fir_taps, band_bins):
    ncols = lax.axis_size("col")
    slots, _, records, _ = raw_files.shape
    packet = whiten(raw_files, file_channels, reader_counts, fir_taps, band_bins, ncols)
    packets = [block for _, block in shifted(packet, "row", ROW_ORDER)]
    own = own_block(packets, records, slots)
    lefts = shifted(own, "col", COL_ORDER)
    lefts = [lefts[0]] + sorted(lefts[1:], key=lambda left: USE_ORDER.index(left[0]) if left[0] in USE_ORDER else 9)
    return stacked(packets, lefts, records, slots)[:, None, :, :]


def solution(mesh):
    return jax.shard_map(
        on_device,
        mesh=mesh,
        in_specs=(
            P(("groups", "row"), "col", None, None),
            P(("groups", "row"), "col"),
            P(("groups", "row"), "col"),
            P(),
            P(),
        ),
        out_specs=P(("groups", "row"), "col", None, None),
        check_vma=False,
    )
```

```python
import functools

import jax
import jax.numpy as jnp
from jax import lax
from jax.experimental import pallas as pl
from jax.experimental.pallas import tpu as pltpu
from jax.sharding import PartitionSpec as P


CH_DEV = 16
DEC = 4
SPAN = 1024
LANES = 128
TILE = 16
BLOCK = 64
EARLY = 2
CHAINS = 4
PARTS = 1
USE = (0, 1, 3, 2)
GROUP = 128
HALF = 64
CUTS = (4, 8)
MXU = 256
SMALL = 16 << 20
ROW_PLANS = {4: ((1, 0, 3, 2), (3, 2, 0, 1), (2, 3, 1, 0))}
COL_PLANS = {4: ((1, 0, 3, 2), (2, 3, 0, 1), (3, 2, 1, 0))}
SIN = (6.283185307, -41.341702147, 81.60523051, -76.704495669, 42.014104466, -14.423992009)


def split(x):
    high = x.astype(jnp.bfloat16)
    return high, (x - high.astype(jnp.float32)).astype(jnp.bfloat16)


def turn_cos(steps, length):
    steps = steps - jnp.round(steps * (1.0 / length)) * length
    gap = 0.25 - jnp.abs(steps * (1.0 / length))
    square = gap * gap
    value = jnp.full_like(gap, SIN[-1])
    for term in SIN[-2::-1]:
        value = value * square + term
    return value * gap


def dot(a, b):
    return jnp.dot(a, b, preferred_element_type=jnp.float32)


def iota(shape, axis):
    return lax.broadcasted_iota(jnp.int32, shape, axis)


def whiten_kernel(ncols, records, *refs):
    (raw, taps_in, bins_in, channels_in), counts, refs = refs[:4], refs[4:-8], refs[-8:]
    out, held, taps, bins, channels, waves, ordered, sems = refs
    rows, samples = raw.shape
    taps_count = taps.shape[1]
    length = samples // DEC
    blocks = (samples + SPAN - 1) // SPAN
    sets = [range(a, min(b, blocks)) for a, b in zip((0,) + CUTS, CUTS + (blocks,)) if a < blocks]
    small = []
    for index, (source, target) in enumerate(((taps_in, taps), (bins_in, bins), (channels_in, channels))):
        small.append(pltpu.make_async_copy(source, target, sems.at[index]))
        small[-1].start()
    copies = []
    for index, group in enumerate(sets):
        start = group[0] * SPAN
        part = pl.ds(start, min(len(group) * SPAN, samples - start))
        copies.append(pltpu.make_async_copy(raw.at[:, part], held.at[:, part], sems.at[3 + index]))
        copies[-1].start()
    for copy in small:
        copy.wait()
    width = out.shape[1]
    half = width // 2
    before = taps_count // DEC - 1
    tiles = SPAN // LANES
    depth = (LANES // DEC + before + TILE - 1) // TILE * TILE
    quarter = 0.25 * length
    base = bins[...].astype(jnp.float32)
    band = jnp.concatenate([base, base], axis=1)
    turn_at, back_at = depth, depth + tiles
    cos_at = depth + 2 * tiles
    sin_at = cos_at + TILE
    lower = iota((sin_at + TILE, width), 1) // half
    row = iota((sin_at + TILE, width), 0)
    steps = jnp.where(row < turn_at, row - before, (row - turn_at) % tiles * (LANES // DEC))
    steps = jnp.where(row < cos_at, steps, (row - cos_at) % TILE * (SPAN // DEC))
    shift = jnp.where(row < turn_at, lower, 0)
    shift = jnp.where((row >= back_at) & (row < cos_at), 1, shift)
    shift = jnp.where(row >= sin_at, 1, shift)
    values = turn_cos(steps.astype(jnp.float32) * band - shift.astype(jnp.float32) * quarter, length)
    flip = (row >= back_at) & (row < cos_at) & (lower == 0)
    waves[...] = jnp.where(flip, -values, values)
    gap = iota((LANES, LANES), 0) - DEC * (iota((LANES, LANES), 1) - before)
    lane_taps = jnp.concatenate([taps[...], jnp.zeros((1, LANES - taps_count), jnp.float32)], axis=1)
    lane_taps = jnp.broadcast_to(lane_taps, (LANES, LANES))
    banded = jnp.take_along_axis(lane_taps, jnp.clip(gap, 0, taps_count - 1), axis=1)
    banded = jnp.where((gap >= 0) & (gap < taps_count), banded, 0.0)
    edge_rows = (DEC * before + TILE - 1) // TILE * TILE
    early = jnp.where(iota((edge_rows, LANES), 1) < before, -banded[:edge_rows], 0.0)
    filters = jnp.concatenate(split(jnp.concatenate([banded, early], axis=0)), axis=1)
    wave_high, wave_low = split(waves[:depth, :])
    space = jnp.zeros((LANES - depth, 2 * width), jnp.bfloat16)
    rhs = jnp.concatenate(
        [
            jnp.concatenate([wave_high, wave_low], axis=1),
            space,
            jnp.concatenate([wave_high, jnp.zeros_like(wave_low)], axis=1),
            space,
        ],
        axis=0,
    )

    def product(acc):
        pltpu.matmul_push_rhs(rhs, 0, 0)
        pltpu.matmul_acc_lhs(acc, filters, load_staged_rhs=0)
        both = pltpu.matmul_pop(acc)
        return both[:, :width] + both[:, width:]

    filtered = pl.run_scoped(product, pltpu.ACC(0)((LANES + edge_rows, MXU), jnp.float32))
    first, edge = filtered[:LANES], filtered[LANES:]
    swapped = pltpu.roll(first, half, 1)
    half_tables = []
    for index in range(0, tiles, MXU // LANES):
        pieces = []
        for tile in range(index, index + MXU // LANES):
            turned = first * waves[turn_at + tile : turn_at + tile + 1, :]
            turned = turned + swapped * waves[back_at + tile : back_at + tile + 1, :]
            pieces.append(turned if tile else first)
        half_tables.append(jnp.concatenate(split(jnp.concatenate(pieces, axis=0)), axis=1))
    edge = jnp.concatenate(split(edge), axis=1)
    edge = jnp.concatenate([edge, jnp.zeros((MXU - edge_rows, 2 * width), jnp.bfloat16)], axis=0)
    sign = jnp.where(iota((1, width), 1) < half, 1.0, -1.0)
    slots = rows // records

    def piece(part, start):
        size = min(MXU, samples - start)
        block = held[part, start : start + size]
        if size < MXU:
            block = jnp.concatenate([block, jnp.zeros((HALF, MXU - size), block.dtype)], axis=1)
        return block

    accs = [
        pltpu.ACC(block % 2)((HALF, 2 * width), jnp.float32) for block in range(blocks) for _ in range(GROUP // HALF)
    ]

    def finish(top, along, across):
        spectra = along * sign - pltpu.roll(across, half, 1)
        power = jnp.mean(spectra * spectra, axis=1, keepdims=True)
        white = spectra / jnp.sqrt(power + 1e-06)
        if counts:
            slot = (iota((HALF, 1), 0) + top) // records
            white = jnp.where(slot < counts[0][0, 0], white, 0.0)
        for index in range(HALF // records):
            turned = pl.ds(top // records + index, records, stride=slots)
            ordered[turned, :] = white[index * records : (index + 1) * records]

    steps_count = SPAN // MXU

    def used(members, step, unit):
        return [b for b in members if b % 2 == unit and b * SPAN + step * MXU < samples]

    orders = [[step for members in sets for step in range(steps_count) if used(members, step, unit)] for unit in range(2)]

    def push_next(unit, pushed):
        if pushed[unit] < len(orders[unit]):
            pltpu.matmul_push_rhs(half_tables[orders[unit][pushed[unit]]], pushed[unit] % 2, unit)
        pushed[unit] += 1

    def every_group(*accs):
        def pop(block, part, sums):
            both = pltpu.matmul_pop(accs[block * (GROUP // HALF) + part])
            term = both[:, :width] + both[:, width:]
            if block == 0:
                sums[part] = (term, jnp.zeros_like(term))
            else:
                along, across = sums[part]
                along = along + term * waves[cos_at + block : cos_at + block + 1, :]
                across = across + term * waves[sin_at + block : sin_at + block + 1, :]
                sums[part] = (along, across)

        def drain(both, parts, sums):
            for part in range(parts):
                for block in both:
                    pop(block, part, sums)

        for group in range(rows // GROUP):
            tops = [group * GROUP + part * HALF for part in range(GROUP // HALF)]
            sums = [None] * len(tops)
            ready, late = [], []
            pushed = [0, 0]
            pltpu.matmul_push_rhs(edge, 1, 0)
            for unit in range(2):
                push_next(unit, pushed)
            for number, members in enumerate(sets):
                if group == 0:
                    copies[number].wait()
                if number == 0:
                    for part, top in enumerate(tops):
                        lhs = piece(pl.ds(top, HALF), 0)
                        pltpu.matmul_acc_lhs(accs[part], lhs, load_staged_rhs=None if part else 1)
                for step in range(steps_count):
                    fresh = [None, None]
                    for unit in range(2):
                        if used(members, step, unit):
                            fresh[unit] = (pushed[unit] - 1) % 2
                            push_next(unit, pushed)
                    for pair in range(members[0], members[-1] + 1, 2):
                        both = [block for block in (pair, pair + 1) if block in members]
                        for part, top in enumerate(tops):
                            for block in both:
                                start = block * SPAN + step * MXU
                                if start < samples:
                                    acc = accs[block * len(tops) + part]
                                    lhs = piece(pl.ds(top, HALF), start)
                                    pltpu.matmul_acc_lhs(acc, lhs, load_staged_rhs=fresh[block % 2])
                                    fresh[block % 2] = None
                        if ready:
                            drain(ready.pop(0), len(tops), sums)
                        if step == steps_count - 1:
                            late.append(both)
                while ready:
                    drain(ready.pop(0), len(tops), sums)
                ready, late = late, []
            for both in ready:
                drain(both, len(tops), sums)
            for part, top in enumerate(tops):
                finish(top, *sums[part])

    pl.run_scoped(every_group, *accs)
    out[:rows, :] = ordered[...].astype(out.dtype)
    owner = channels[...] // (CH_DEV * ncols)
    local = owner * CH_DEV + channels[...] % CH_DEV
    if counts:
        local = jnp.where(iota((1, slots), 1) < counts[0][0, 0], local, -1)
    local = local.astype(jnp.float32)
    local = jnp.concatenate([local, jnp.zeros((1, LANES - slots), jnp.float32)], axis=1)
    local = jnp.broadcast_to(local, (TILE, LANES))
    labels = jnp.take_along_axis(local, iota((TILE, LANES), 1) % slots, axis=1)
    out[rows:, :] = labels.astype(out.dtype)


def whiten(raw_files, file_channels, reader_counts, fir_taps, band_bins, ncols):
    slots, _, records, samples = raw_files.shape
    rows = slots * records
    bins = band_bins.shape[0]
    taps = fir_taps.shape[0]
    width = 2 * bins
    counts = [] if slots == CH_DEV else [reader_counts]
    anywhere = pl.BlockSpec(memory_space=pl.ANY)
    depth = (LANES // DEC + taps // DEC - 1 + TILE - 1) // TILE * TILE
    table_rows = depth + 2 * (SPAN // LANES) + 2 * TILE
    return pl.pallas_call(
        functools.partial(whiten_kernel, ncols, records),
        out_shape=jax.ShapeDtypeStruct((rows + TILE, width), jnp.bfloat16),
        in_specs=[anywhere] * 4 + [pl.BlockSpec(memory_space=pltpu.SMEM)] * len(counts),
        out_specs=pl.BlockSpec(memory_space=pltpu.VMEM),
        scratch_shapes=[
            pltpu.VMEM((rows, samples), jnp.bfloat16),
            pltpu.VMEM((1, taps), jnp.float32),
            pltpu.VMEM((1, bins), jnp.int32),
            pltpu.VMEM((1, slots), jnp.int32),
            pltpu.VMEM((table_rows, width), jnp.float32),
            pltpu.VMEM((rows, width), jnp.float32),
            pltpu.SemaphoreType.DMA((len(CUTS) + 4,)),
        ],
        compiler_params=pltpu.CompilerParams(vmem_limit_bytes=SMALL),
        cost_estimate=pl.CostEstimate(
            flops=4 * rows * samples * width, bytes_accessed=2 * rows * samples, transcendentals=0
        ),
        name="whiten",
    )(
        *(
            pltpu.with_memory_space_constraint(x, pltpu.HBM)
            for x in (
                raw_files.reshape(rows, samples),
                fir_taps.reshape(1, -1),
                band_bins.reshape(1, -1),
                file_channels.reshape(1, -1),
            )
        ),
        *counts,
    )


def gather_channels(packets, first, count, slots, records):
    held = LANES // slots
    picks = []
    for start in range(0, len(packets), held):
        group = packets[start : start + held]
        lane = iota((1, LANES), 1) // slots
        label = jnp.full((1, LANES), -1.0, jnp.float32)
        for index, packet in enumerate(group):
            row = packet[slots * records : slots * records + TILE, :].astype(jnp.float32)[:1]
            label = jnp.where(lane == index, row, label)
        wanted = (iota((count, 1), 0) + first).astype(jnp.float32)
        pick = (wanted == label).astype(jnp.float32).astype(jnp.bfloat16)
        picks.append(pick[:, : len(group) * slots])
    data = [
        jnp.concatenate([packet[e * slots : (e + 1) * slots, :] for e in range(records)], axis=1)
        for packet in packets
    ]
    return dot(jnp.concatenate(picks, axis=1), jnp.concatenate(data, axis=0))


def own_kernel(records, slots, *refs):
    packets, out = refs[:-1], refs[-1]
    width = out.shape[1]
    placed = gather_channels(packets, lax.axis_index("row") * CH_DEV, CH_DEV, slots, records)
    for e in range(records):
        out[e * CH_DEV : (e + 1) * CH_DEV, :] = placed[:, e * width : (e + 1) * width].astype(out.dtype)


def own_block(packets, records, slots):
    vmem = pl.BlockSpec(memory_space=pltpu.VMEM)
    return pl.pallas_call(
        functools.partial(own_kernel, records, slots),
        out_shape=jax.ShapeDtypeStruct((CH_DEV * records, packets[0].shape[1]), packets[0].dtype),
        in_specs=[vmem] * len(packets),
        out_specs=vmem,
        compiler_params=pltpu.CompilerParams(vmem_limit_bytes=SMALL),
        name="own",
    )(*packets)


def stack_piece(records, left, right_re, right_im, turned, tile, send=None):
    width = left.shape[1]
    half = width // 2
    count = right_re.shape[1]
    low = iota((1, width), 1) < half
    piece = left[...].astype(jnp.float32) * (1.0 / records)
    swapped = pltpu.roll(piece, half, 1)
    turned[0] = piece
    turned[1] = jnp.where(low, swapped, -swapped)

    def some(first, number):
        @pl.loop(0, count // BLOCK)
        def _(j):
            rows = pl.ds(pl.multiple_of(j * BLOCK, BLOCK), BLOCK)
            res = [right_re[e, rows, :] for e in range(records)]
            ims = [right_im[e, rows, :] for e in range(records)]
            for k in range(first, first + number):
                terms = [None] * CHAINS
                for e in range(records):
                    at = slice(e * CH_DEV + k, e * CH_DEV + k + 1)
                    for side, right in ((0, res[e]), (1, ims[e])):
                        wide = jnp.broadcast_to(turned[side, at, :], (TILE, width)).astype(jnp.bfloat16)
                        term = jnp.concatenate([wide] * (BLOCK // TILE), axis=0) * right
                        chain = (2 * e + side) % CHAINS
                        terms[chain] = term if terms[chain] is None else terms[chain] + term
                while len(terms) > 1:
                    terms = [a + b for a, b in zip(terms[::2], terms[1::2])] + terms[len(terms) // 2 * 2 :]
                tile[k, rows, :] = terms[0]

    if send is None:
        some(0, CH_DEV)
    else:
        for first in range(0, CH_DEV, CH_DEV // PARTS):
            some(first, CH_DEV // PARTS)
            send(first, CH_DEV // PARTS)


def first_kernel(records, slots, *refs):
    packets = refs[:-5]
    left, tile, right_re, right_im, turned = refs[-5:]
    width = left.shape[1]
    half = width // 2
    count = right_re.shape[1]
    low = iota((1, width), 1) < half
    for start in range(0, count, BLOCK):
        placed = gather_channels(packets, start, BLOCK, slots, records)
        for e in range(records):
            one = placed[:, e * width : (e + 1) * width]
            swapped = pltpu.roll(one, half, 1)
            right_re[e, start : start + BLOCK, :] = jnp.where(low, one, swapped).astype(right_re.dtype)
            right_im[e, start : start + BLOCK, :] = jnp.where(low, swapped, one).astype(right_im.dtype)
    stack_piece(records, left, right_re, right_im, turned, tile)


def next_kernel(records, left, right_re, right_im, after, tile, turned):
    del after
    stack_piece(records, left, right_re, right_im, turned, tile)


def last_kernel(records, plans, made, *refs):
    done, refs = refs[:made], refs[made:]
    lefts, refs = refs[: len(plans) - made], refs[len(plans) - made :]
    right_re, right_im, out, turned, tiles, sems = refs
    mine = lax.axis_index("col")
    copies = []

    def send(tile, index, first, number):
        start = source_of(mine, plans[index]) * CH_DEV + first
        sem = sems.at[index, first * PARTS // CH_DEV]
        copies.append(pltpu.make_async_copy(tile.at[pl.ds(first, number)], out.at[pl.ds(start, number)], sem))
        copies[-1].start()

    for index, tile in enumerate(done):
        send(tile, index, 0, CH_DEV)
    for index, left in enumerate(lefts):
        tile = tiles.at[index]
        stack_piece(
            records, left, right_re, right_im, turned, tile, functools.partial(send, tile, made + index)
        )
    for copy in copies:
        copy.wait()


def stacked(packets, lefts, records, slots):
    nrows, ncols = len(packets), len(lefts)
    width = packets[0].shape[1]
    count = nrows * CH_DEV
    vmem = pl.BlockSpec(memory_space=pltpu.VMEM)
    right = jax.ShapeDtypeStruct((records, count, width), jnp.bfloat16)
    tile = jax.ShapeDtypeStruct((CH_DEV, count, width), jnp.bfloat16)
    turned = pltpu.VMEM((2, CH_DEV * records, width), jnp.float32)
    params = pltpu.CompilerParams(vmem_limit_bytes=SMALL)

    def cost(pieces):
        work = 4 * CH_DEV * count * width * records * pieces
        return pl.CostEstimate(flops=256 * work, bytes_accessed=tile.size * 2 * pieces, transcendentals=0)

    first, right_re, right_im = pl.pallas_call(
        functools.partial(first_kernel, records, slots),
        out_shape=(tile, right, right),
        in_specs=[vmem] * (nrows + 1),
        out_specs=(vmem,) * 3,
        scratch_shapes=[turned],
        compiler_params=params,
        cost_estimate=cost(1),
        name="first",
    )(*packets, lefts[0][1])
    tiles = [first]
    early = min(EARLY, ncols - 2)
    for _, left in lefts[1 : 1 + early]:
        tiles.append(
            pl.pallas_call(
                functools.partial(next_kernel, records),
                out_shape=tile,
                in_specs=[vmem] * 3 + [pl.BlockSpec(memory_space=pl.ANY)],
                out_specs=vmem,
                scratch_shapes=[turned],
                compiler_params=params,
                cost_estimate=cost(1),
                name="next",
            )(left, right_re, right_im, tiles[-1])
        )
    others = [left for _, left in lefts[1 + early :]]
    return pl.pallas_call(
        functools.partial(last_kernel, records, [targets for targets, _ in lefts], len(tiles)),
        out_shape=jax.ShapeDtypeStruct((ncols * CH_DEV, count, width), jnp.bfloat16),
        in_specs=[vmem] * (len(tiles) + len(others) + 2),
        out_specs=pl.BlockSpec(memory_space=pl.ANY),
        scratch_shapes=[
            turned,
            pltpu.VMEM((len(others), CH_DEV, count, width), jnp.bfloat16),
            pltpu.SemaphoreType.DMA((ncols, PARTS)),
        ],
        compiler_params=params,
        cost_estimate=cost(len(others)),
        name="last",
    )(*tiles, *others, right_re, right_im)


def plan_of(size, plans):
    if size in plans:
        return plans[size]
    if size & (size - 1) == 0:
        return [[i ^ shift for i in range(size)] for shift in range(1, size)]
    return [[(i + shift) % size for i in range(size)] for shift in range(1, size)]


def source_of(index, targets):
    source = jnp.int32(0)
    for i, target in enumerate(targets):
        source = jnp.where(index == target, jnp.int32(i), source)
    return source


def exchanged(block, axis, plans):
    size = lax.axis_size(axis)
    return [(list(range(size)), block)] + [(targets, moved(block, axis, targets)) for targets in plan_of(size, plans)]


def moved(block, axis, targets):
    return lax.ppermute(block, axis, list(enumerate(targets)))


def on_device(raw_files, file_channels, reader_counts, fir_taps, band_bins):
    ncols = lax.axis_size("col")
    slots, _, records, _ = raw_files.shape
    packet = whiten(raw_files, file_channels, reader_counts, fir_taps, band_bins, ncols)
    packets = [block for _, block in exchanged(packet, "row", ROW_PLANS)]
    own = own_block(packets, records, slots)
    lefts = exchanged(own, "col", COL_PLANS)
    if ncols in COL_PLANS:
        lefts = [lefts[n] for n in USE]
    return stacked(packets, lefts, records, slots)[:, None, :, :]


def solution(mesh):
    return jax.shard_map(
        on_device,
        mesh=mesh,
        in_specs=(
            P(("groups", "row"), "col", None, None),
            P(("groups", "row"), "col"),
            P(("groups", "row"), "col"),
            P(),
            P(),
        ),
        out_specs=P(("groups", "row"), "col", None, None),
        check_vma=False,
    )
```
